32 devices in a mesh: tm: 2 (over x), grid: 16 (over z, y, core).
Axes of the slice: x: 2, y: 2, z: 4, core: 2. Of those that a mesh axis runs over, the one named last changes fastest.
Arguments:
- occupied_green: bfloat16 [2, 1024, 1024], P('tm', 'grid'), may hold values from -0.005859375 to 0.005859375
- empty_green: bfloat16 [2, 1024, 1024], P('tm', 'grid'), may hold values from -0.005859375 to 0.005859375
- basis: bfloat16 [12288, 1024], P('grid'), may hold values from -8 to 8
- time_weights: float32 [2, 2], replicated, may hold values from 0.25 to 1
Outputs:
- polarizability: float32 [2, 1024, 1024], P('tm', 'grid')
The draws below stay inside these ranges and needn't reach their ends.
All inputs are finite; a program needn't handle non-finite values.
Results may differ from the reference program's by a relative error of at most 0.0012.
Values may be sent and summed in bfloat16 or wider, within the bound.
A program may use at most 128 MiB of HBM per device.

```python
import math
import jax
import jax.numpy as jnp
from jax import lax

NR = 12288
NB = 1024
TIMES = 2
FREQS = 2


def draw_basis(key, part):
    draw_keys = jax.random.split(jax.random.fold_in(key, 7103), 5)
    positions = jnp.arange(NR, dtype=jnp.float32)[:, None]
    centres = jax.random.uniform(draw_keys[0], (1, NB), jnp.float32, 0.0, float(NR))
    spreads = jnp.exp(jax.random.uniform(draw_keys[1], (1, NB), jnp.float32, math.log(2.0 * NR / NB), math.log(NR / 8.0)))
    offsets = jnp.abs(positions - centres)
    distance = jnp.minimum(offsets, float(NR) - offsets)
    wavenumber = jax.random.uniform(draw_keys[2], (1, NB), jnp.float32, 0.5, 3.0) * (2.0 * math.pi) / spreads
    phases = jax.random.uniform(draw_keys[3], (1, NB), jnp.float32, -math.pi, math.pi)
    relative = distance / spreads
    envelope = 0.2 + 1.0 / (1.0 + relative * relative)
    profile = envelope * jnp.cos(wavenumber * distance + phases)
    roughness = jax.random.uniform(draw_keys[4], (NR, NB), jnp.float32, 0.5, 1.5)
    unscaled = profile * roughness
    rms_value = jnp.sqrt(jnp.mean(unscaled * unscaled))
    return jnp.clip(unscaled / rms_value, -8.0, 8.0).astype(jnp.bfloat16)


def level_of(rng, extent, cuts, least, largest):
    def one(dim, blocks):
        steps = jax.random.uniform(jax.random.fold_in(jax.random.fold_in(rng, 6), dim), (blocks,), jnp.float32, least / len(cuts), largest / len(cuts))
        return jnp.repeat(jnp.exp(steps), extent[dim] // blocks).reshape((-1,) + (1,) * (len(extent) - dim - 1))

    factor_of = one(*cuts[0])
    for cut in cuts[1:]:
        factor_of = factor_of * one(*cut)
    return factor_of


def normal_values(key, shape, spread, limit, pieces=(), kind=jnp.bfloat16):
    entries = spread * jax.random.normal(key, shape, jnp.float32)
    if pieces:
        entries = entries * level_of(key, shape, pieces, -0.22, 0.18)
    return jnp.clip(entries, -limit, limit).astype(kind)


def setup_inputs(seed: int = 0) -> dict:
    streams_of = jax.random.split(jax.random.key(seed), 5)
    return {
        "occupied_green": normal_values(streams_of[0], (TIMES, NB, NB), (NB * NB) ** -0.5, 0.005859375, ((0, 2), (1, 16))),
        "empty_green": normal_values(streams_of[1], (TIMES, NB, NB), (NB * NB) ** -0.5, 0.005859375, ((0, 2), (1, 16))),
        "basis": draw_basis(jax.random.fold_in(streams_of[4], 71), 0),
        "time_weights": jnp.clip(jax.random.uniform(streams_of[3], (FREQS, TIMES), jnp.float32, 0.25, 1.0), 0.25, 1.0),
    }


def reference(occupied_green, empty_green, basis, time_weights):
    block_rows = math.gcd(NR, 2048)
    block_total = NR // block_rows
    scale_factor = 1.0 / NR
    totals = []
    for time_increment in range(TIMES):
        occupied_now = occupied_green[time_increment]
        empty_now = empty_green[time_increment]

        def one_block(block_index):
            local_rows = lax.dynamic_slice_in_dim(basis, block_index * block_rows, block_rows, 0)
            occ_proj = jnp.dot(local_rows, occupied_now.T, preferred_element_type=jnp.float32).astype(jnp.bfloat16)
            emp_proj = jnp.dot(local_rows, empty_now.T, preferred_element_type=jnp.float32).astype(jnp.bfloat16)
            occ_real = jnp.dot(occ_proj, basis.T, preferred_element_type=jnp.float32)
            emp_real = jnp.dot(emp_proj, basis.T, preferred_element_type=jnp.float32)
            product = (occ_real * emp_real).astype(jnp.bfloat16)
            back_half = jnp.dot(product, basis, preferred_element_type=jnp.float32).astype(jnp.bfloat16)
            return jnp.dot(back_half.T, local_rows, preferred_element_type=jnp.float32)

        partial_sets = lax.map(one_block, jnp.arange(block_total, dtype=jnp.int32))
        totals.append(jnp.sum(partial_sets, axis=0))
    result_list = []
    for freq_step in range(FREQS):
        accum = jnp.zeros((NB, NB), jnp.float32)
        for time_increment in range(TIMES):
            accum = accum + time_weights[freq_step, time_increment] * totals[time_increment]
        result_list.append(scale_factor * accum)
    return jnp.stack(result_list)
```

```python
import functools

import jax
import jax.numpy as jnp
from jax import lax
from jax.experimental import pallas as pl
from jax.experimental.pallas import tpu as pltpu
from jax.sharding import PartitionSpec as P

MESH = pl.DeviceIdType.MESH
NT = (((1,), (1,)), ((), ()))
TN = (((0,), (0,)), ((), ()))


def tile_of(total, most):
    return max(d for d in range(1, most + 1) if total % d == 0)


def kernel(
    nc, nr, occ_ref, emp_ref, basis_ref, w_ref, out_ref,
    full, green, proj, acc, part, half, sums, twin,
    load_sem, gs_ring, gr_ring, gs_loc, gr_loc,
    s_ring, r_ring, s_x, r_x, s_loc, r_loc,
    cs_sem, cr_sem, ss_sem, sr_sem, ts_sem, tr_sem,
):
    tm = lax.axis_index("tm")
    me = lax.axis_index("grid")
    rows, nb = basis_ref.shape
    kb = occ_ref.shape[1]
    core = lax.rem(me, 2)
    chip = me // 2
    side = lax.rem(chip, 2)
    lane = chip // 2
    pos = (1 - side) * lane + side * (nc - 1 - lane)
    step_dir = 1 - 2 * core

    def chip_at(position):
        q = lax.rem(position + 2 * nc, nc)
        far = q // (nc // 2)
        return (1 - far) * 2 * q + far * (2 * (nc - 1 - q) + 1)

    def block_at(hops, which_core):
        direction = 1 - 2 * which_core
        return 2 * chip_at(pos - direction * hops) + which_core

    nxt = (tm, 2 * chip_at(pos + step_dir) + core)
    prv = (tm, 2 * chip_at(pos - step_dir) + core)
    mate = (tm, me + step_dir)
    other = (1 - tm, me)
    mate_core = 1 - core

    def remote(src, dst, send, recv, dev):
        return pltpu.make_async_remote_copy(
            src_ref=src, dst_ref=dst, send_sem=send, recv_sem=recv, device_id=dev, device_id_type=MESH
        )

    loads = [
        pltpu.make_async_copy(occ_ref.at[0], green.at[me, 0], load_sem.at[0]),
        pltpu.make_async_copy(emp_ref.at[0], green.at[me, 1], load_sem.at[1]),
        pltpu.make_async_copy(basis_ref, full.at[me], load_sem.at[2]),
    ]
    for load in loads:
        load.start()

    barrier = pltpu.get_barrier_semaphore()
    for peer in (nxt, prv, mate, other):
        pl.semaphore_signal(barrier, inc=1, device_id=peer, device_id_type=MESH)
    pl.semaphore_wait(barrier, 4)

    def g_ring(hops, u):
        b = block_at(hops, core)
        return remote(green.at[b, u], green.at[b, u], gs_ring.at[2 * hops + u], gr_ring.at[2 * hops + u], nxt)

    def g_loc(hops, u, which_core):
        b = block_at(hops, which_core)
        return remote(green.at[b, u], green.at[b, u], gs_loc.at[2 * hops + u], gr_loc.at[2 * hops + u], mate)

    def g_arrived(hops, u):
        b = block_at(hops, core)
        return remote(
            green.at[b, u], green.at[b, u], gs_ring.at[2 * (hops - 1) + u], gr_ring.at[2 * (hops - 1) + u], nxt
        )

    third = rows // 3

    def piece(b, t):
        return full.at[b, pl.ds(pl.multiple_of(t * third, 16), third)]

    def third_of(u):
        return (2 * tm, 1, 2 - 2 * tm)[u]

    def b_ring(hops, u, src_hops):
        ref = piece(block_at(src_hops, core), third_of(u))
        return remote(ref, ref, s_ring.at[2 * hops + u], r_ring.at[2 * hops + u], nxt)

    def b_x(hops, u):
        ref = piece(block_at(hops, core), third_of(u))
        return remote(ref, ref, s_x.at[hops], r_x.at[hops], other)

    def b_loc(hops, u, which_core):
        ref = piece(block_at(hops, which_core), third_of(u))
        return remote(ref, ref, s_loc.at[3 * hops + u], r_loc.at[3 * hops + u], mate)

    for u in range(2):
        loads[u].wait()
        g_ring(0, u).start()
        g_loc(0, u, core).start()
    loads[2].wait()
    for u in range(3):
        b_loc(0, u, core).start()

    def g_step(s, carry):
        for u in range(2):
            g_arrived(s, u).wait_recv()

            @pl.when(s < nc - 1)
            def _():
                g_ring(s, u).start()

            g_loc(s, u, core).start()
        return carry

    lax.fori_loop(1, nc, g_step, 0)
    for u in range(2):
        b_ring(0, u, 0).start()

    def g_local(s, carry):
        for u in range(2):
            g_loc(s, u, mate_core).wait_recv()
        return carry

    lax.fori_loop(0, nc, g_local, 0)

    per = tile_of(2 * nc, max(1, 256 // kb))
    tiles = 2 * nc // per

    def project(i, carry):
        f = i // tiles
        j = lax.rem(i, tiles)
        g = green[pl.ds(j * per, per), f].reshape(per * kb, nb)
        res = lax.dot_general(full[me], g, NT, preferred_element_type=jnp.float32)
        proj[f, :, pl.ds(pl.multiple_of(j * per * kb, 128), per * kb)] = res.astype(jnp.bfloat16)
        return carry

    lax.fori_loop(0, 2 * tiles, project, 0)
    acc[...] = jnp.zeros_like(acc)

    tile = tile_of(rows, 256)

    def compute(b):
        def one(i, carry):
            sub = full[b, pl.ds(pl.multiple_of(i * tile, 16), tile), :]
            occ = lax.dot_general(proj[0], sub, NT, preferred_element_type=jnp.float32)
            emp = lax.dot_general(proj[1], sub, NT, preferred_element_type=jnp.float32)
            product = (occ * emp).astype(jnp.bfloat16)
            acc[...] += jnp.dot(product, sub, preferred_element_type=jnp.float32)
            return carry

        lax.fori_loop(0, rows // tile, one, 0)

    def step(s, carry):
        @pl.when(s < nc)
        def _():
            b_ring(s - 1, 0, s).wait_recv()

            @pl.when(s < nc - 1)
            def _():
                b_ring(s, 0, s).start()

            b_x(s, 0).start()
            b_loc(s, 0, core).start()

        @pl.when(s > 1)
        def _():
            b_x(s - 1, 2).wait_recv()
            b_loc(s - 1, 2, core).start()

        compute(block_at(s - 1, core))

        @pl.when(s < nc)
        def _():
            b_ring(s - 1, 1, s).wait_recv()

            @pl.when(s < nc - 1)
            def _():
                b_ring(s, 1, s).start()

            b_loc(s, 1, core).start()

        for u in range(3):
            b_loc(s - 1, u, mate_core).wait_recv()
        compute(block_at(s - 1, mate_core))
        return carry

    lax.fori_loop(1, nc + 1, step, 0)

    cper = tile_of(nc, max(1, 128 // kb))
    ctiles = nc // cper

    def coef_copy(j):
        q = pl.ds(j * cper, cper)
        return remote(part.at[mate_core, q], half.at[q], cs_sem.at[j], cr_sem.at[j], mate)

    def coef(j, carry):
        cols = 2 * cper * kb
        back = acc[:, pl.ds(pl.multiple_of(j * cols, 128), cols)].astype(jnp.bfloat16)
        res = lax.dot_general(back, full[me], TN, preferred_element_type=jnp.float32)
        for i in range(2 * cper):
            part[i % 2, j * cper + i // 2] = res[i * kb:(i + 1) * kb]
        coef_copy(j).start()
        return carry

    lax.fori_loop(0, ctiles, coef, 0)

    def coef_wait(j, carry):
        coef_copy(j).wait_recv()
        q = pl.ds(j * cper, cper)
        part[core, q] = part[core, q] + half[q]
        return carry

    lax.fori_loop(0, ctiles, coef_wait, 0)

    hk = kb // 2

    def rs_copy(s, u):
        q = chip_at(pos - step_dir * (1 + s))
        return remote(
            part.at[core, q, pl.ds(u * hk, hk)], sums.at[s, pl.ds(u * hk, hk)],
            ss_sem.at[2 * s + u], sr_sem.at[2 * s + u], nxt,
        )

    for u in range(2):
        rs_copy(0, u).start()

    def rs_step(s, carry):
        q = chip_at(pos - step_dir * (1 + s))
        for u in range(2):
            rs_copy(s - 1, u).wait_recv()
            span = pl.ds(u * hk, hk)
            part[core, q, span] = part[core, q, span] + sums[s - 1, span]
            rs_copy(s, u).start()
        return carry

    lax.fori_loop(1, nc - 1, rs_step, 0)

    def tm_copy(u):
        span = pl.ds(u * hk, hk)
        return remote(part.at[core, chip, span], twin.at[span], ts_sem.at[u], tr_sem.at[u], other)

    for u in range(2):
        rs_copy(nc - 2, u).wait_recv()
        span = pl.ds(u * hk, hk)
        part[core, chip, span] = part[core, chip, span] + sums[nc - 2, span]
        tm_copy(u).start()
    scale = 1.0 / nr
    for u in range(2):
        tm_copy(u).wait_recv()
        span = pl.ds(u * hk, hk)
        mine = w_ref[tm, tm] * part[core, chip, span]
        out_ref[0, span] = scale * (mine + w_ref[tm, 1 - tm] * twin[span])

    def drain(s, carry):
        for u in range(2):
            @pl.when(s < nc - 1)
            def _():
                g_ring(s, u).wait_send()
                b_ring(s, u, s).wait_send()
                rs_copy(s, u).wait_send()

            g_loc(s, u, core).wait_send()
        for u in range(3):
            b_loc(s, u, core).wait_send()

        @pl.when(s > 0)
        def _():
            b_x(s, 0).wait_send()

        return carry

    lax.fori_loop(0, nc, drain, 0)

    def drain_coef(j, carry):
        coef_copy(j).wait_send()
        return carry

    lax.fori_loop(0, ctiles, drain_coef, 0)
    for u in range(2):
        tm_copy(u).wait_send()


def shards(occupied_green, empty_green, basis, time_weights):
    n = lax.axis_size("grid")
    nc = n // 2
    rows, nb = basis.shape
    kb = occupied_green.shape[1]
    dma = pltpu.SemaphoreType.DMA
    sizes = [3, 2 * nc, 2 * nc, 2 * nc, 2 * nc, 2 * nc, 2 * nc, nc, nc, 3 * nc, 3 * nc]
    sizes += [nc, nc, 2 * nc, 2 * nc, 2, 2]
    any_space = pl.BlockSpec(memory_space=pl.ANY)
    return pl.pallas_call(
        functools.partial(kernel, nc, n * rows),
        out_shape=jax.ShapeDtypeStruct((1, kb, nb), jnp.float32),
        in_specs=[any_space, any_space, any_space, pl.BlockSpec(memory_space=pltpu.SMEM)],
        out_specs=pl.BlockSpec(memory_space=pltpu.VMEM),
        scratch_shapes=[
            pltpu.VMEM((n, rows, nb), jnp.bfloat16),
            pltpu.VMEM((n, 2, kb, nb), jnp.bfloat16),
            pltpu.VMEM((2, rows, nb), jnp.bfloat16),
            pltpu.VMEM((rows, nb), jnp.float32),
            pltpu.VMEM((2, nc, kb, nb), jnp.float32),
            pltpu.VMEM((nc, kb, nb), jnp.float32),
            pltpu.VMEM((nc - 1, kb, nb), jnp.float32),
            pltpu.VMEM((kb, nb), jnp.float32),
        ]
        + [dma((k,)) for k in sizes],
        compiler_params=pltpu.CompilerParams(
            collective_id=0, has_side_effects=True, vmem_limit_bytes=67043328
        ),
    )(occupied_green, empty_green, basis, time_weights)


def solution(mesh):
    in_specs = (P("tm", "grid", None), P("tm", "grid", None), P("grid", None), P())
    out_specs = P("tm", "grid", None)
    return jax.shard_map(shards, mesh=mesh, in_specs=in_specs, out_specs=out_specs, check_vma=False)
```

```python
import functools

import jax
import jax.numpy as jnp
from jax import lax
from jax.experimental import pallas as pl
from jax.experimental.pallas import tpu as pltpu
from jax.sharding import PartitionSpec as P

MESH = pl.DeviceIdType.MESH
NT = (((1,), (1,)), ((), ()))
TN = (((0,), (0,)), ((), ()))


def tile_of(total, most):
    return max(d for d in range(1, most + 1) if total % d == 0)


def kernel(
    nc, nr, occ_ref, emp_ref, basis_ref, w_ref, out_ref,
    full, green, proj, acc, back, part, half, sums, twin,
    load_sem, gs_ring, gr_ring, gs_loc, gr_loc,
    s_ring, r_ring, s_x, r_x, s_loc, r_loc,
    cs_sem, cr_sem, ss_sem, sr_sem, ts_sem, tr_sem,
):
    tm = lax.axis_index("tm")
    me = lax.axis_index("grid")
    rows, nb = basis_ref.shape
    kb = occ_ref.shape[1]
    core = lax.rem(me, 2)
    chip = me // 2
    side = lax.rem(chip, 2)
    lane = chip // 2
    pos = (1 - side) * lane + side * (nc - 1 - lane)
    step_dir = 1 - 2 * core

    def chip_at(position):
        q = lax.rem(position + 2 * nc, nc)
        far = q // (nc // 2)
        return (1 - far) * 2 * q + far * (2 * (nc - 1 - q) + 1)

    def block_at(hops, which_core):
        direction = 1 - 2 * which_core
        return 2 * chip_at(pos - direction * hops) + which_core

    nxt = (tm, 2 * chip_at(pos + step_dir) + core)
    prv = (tm, 2 * chip_at(pos - step_dir) + core)
    mate = (tm, me + step_dir)
    other = (1 - tm, me)
    mate_core = 1 - core

    def remote(src, dst, send, recv, dev):
        return pltpu.make_async_remote_copy(
            src_ref=src, dst_ref=dst, send_sem=send, recv_sem=recv, device_id=dev, device_id_type=MESH
        )

    loads = [
        pltpu.make_async_copy(occ_ref.at[0], green.at[me, 0], load_sem.at[0]),
        pltpu.make_async_copy(emp_ref.at[0], green.at[me, 1], load_sem.at[1]),
        pltpu.make_async_copy(basis_ref, full.at[me], load_sem.at[2]),
    ]
    for load in loads:
        load.start()

    barrier = pltpu.get_barrier_semaphore()
    for peer in (nxt, prv, mate, other):
        pl.semaphore_signal(barrier, inc=1, device_id=peer, device_id_type=MESH)
    pl.semaphore_wait(barrier, 4)

    def g_ring(hops, u):
        b = block_at(hops, core)
        return remote(green.at[b, u], green.at[b, u], gs_ring.at[2 * hops + u], gr_ring.at[2 * hops + u], nxt)

    def g_loc(hops, u, which_core):
        b = block_at(hops, which_core)
        return remote(green.at[b, u], green.at[b, u], gs_loc.at[2 * hops + u], gr_loc.at[2 * hops + u], mate)

    def g_arrived(hops, u):
        b = block_at(hops, core)
        return remote(
            green.at[b, u], green.at[b, u], gs_ring.at[2 * (hops - 1) + u], gr_ring.at[2 * (hops - 1) + u], nxt
        )

    third = rows // 3
    nh = nc // 2

    def piece(b, t):
        return full.at[b, pl.ds(pl.multiple_of(t * third, 16), third)]

    def third_of(u):
        return (2 * tm, 1, 2 - 2 * tm)[u]

    chunk = max(16, 2 * third // nc)
    per_unit = third // chunk

    def own_chunk(c):
        u = c // per_unit
        first = (2 * tm * (1 - u) + u) * third + lax.rem(c, per_unit) * chunk
        ref = full.at[me, pl.ds(pl.multiple_of(first, 16), chunk)]
        remote(ref, ref, s_ring.at[u], r_ring.at[u], nxt).start()

    def b_ring(hops, u, src_hops):
        ref = piece(block_at(src_hops, core), third_of(u))
        return remote(ref, ref, s_ring.at[2 * hops + u], r_ring.at[2 * hops + u], nxt)

    def b_x(hops, u):
        ref = piece(block_at(hops, core), third_of(u))
        return remote(ref, ref, s_x.at[hops], r_x.at[hops], other)

    def b_loc(hops, u, which_core):
        ref = piece(block_at(hops, which_core), third_of(u))
        return remote(ref, ref, s_loc.at[3 * hops + u], r_loc.at[3 * hops + u], mate)

    for u in range(2):
        loads[u].wait()
        g_ring(0, u).start()
        g_loc(0, u, core).start()
    loads[2].wait()
    for u in range(3):
        b_loc(0, u, core).start()
    own_chunk(jnp.int32(0))

    def g_step(s, carry):
        for u in range(2):
            g_arrived(s, u).wait_recv()

            @pl.when(s < nc - 1)
            def _():
                g_ring(s, u).start()

            g_loc(s, u, core).start()

        @pl.when(s < 2 * per_unit)
        def _():
            own_chunk(s)

        return carry

    lax.fori_loop(1, nc, g_step, 0)

    def ring_in(s, u):
        b_ring(s - 1, u, s).wait_recv()

        @pl.when(s < nh)
        def _():
            b_ring(s, u, s).start()
            b_loc(s, u, core).start()

        if u == 0:
            b_x(s, 0).start()

    for u in range(2):
        ring_in(1, u)

    def g_local(s, carry):
        for u in range(2):
            g_loc(s, u, mate_core).wait_recv()
        return carry

    lax.fori_loop(0, nc, g_local, 0)

    per = tile_of(2 * nc, max(1, 256 // kb))
    tiles = 2 * nc // per

    def project(b, i):
        f = i // tiles
        j = lax.rem(i, tiles)
        g = green[pl.ds(j * per, per), f].reshape(per * kb, nb)
        res = lax.dot_general(full[b], g, NT, preferred_element_type=jnp.float32)
        proj[f, :, pl.ds(pl.multiple_of(j * per * kb, 128), per * kb)] = res.astype(jnp.bfloat16)


    tile = tile_of(rows, 768)

    def terms(sub):
        occ = lax.dot_general(proj[0], sub, NT, preferred_element_type=jnp.float32)
        emp = lax.dot_general(proj[1], sub, NT, preferred_element_type=jnp.float32)
        product = (occ * emp).astype(jnp.bfloat16)
        acc[...] += jnp.dot(product, sub, preferred_element_type=jnp.float32)

    def compute(b):
        for i in range(rows // tile):
            terms(full[b, i * tile:(i + 1) * tile])

    def rows_of(which, carry):
        b = block_at(which * nh, core)

        @pl.when(which == 1)
        def _():
            b_x(nh, 2).wait_recv()

        lax.fori_loop(0, 2 * tiles, lambda i, c: (project(b, i), c)[1], 0)
        acc[...] = jnp.zeros_like(acc)

        def step(s, carry):
            first = which == 0

            @pl.when(first & (s > 0))
            def _():
                b_x(s, 2).wait_recv()
                b_loc(s, 2, core).start()

            compute(block_at(s, core))

            @pl.when(first & (s < nh - 1))
            def _():
                ring_in(s + 2, 0)

            @pl.when(first)
            def _():
                for u in range(3):
                    b_loc(s, u, mate_core).wait_recv()

            compute(block_at(s, mate_core))

            @pl.when(first & (s < nh - 1))
            def _():
                ring_in(s + 2, 1)

            return carry

        lax.fori_loop(0, nh, step, 0)
        back[which] = acc[...].astype(jnp.bfloat16)
        return carry

    lax.fori_loop(0, 2, rows_of, 0)

    cper = tile_of(nc, max(1, 128 // kb))
    ctiles = nc // cper

    def coef_copy(j):
        q = pl.ds(j * cper, cper)
        return remote(part.at[mate_core, q], half.at[q], cs_sem.at[j], cr_sem.at[j], mate)

    def coef(j, carry):
        cols = 2 * cper * kb
        span = pl.ds(pl.multiple_of(j * cols, 128), cols)
        res = lax.dot_general(back[0, :, span], full[me], TN, preferred_element_type=jnp.float32)
        far = full[block_at(nh, core)]
        res += lax.dot_general(back[1, :, span], far, TN, preferred_element_type=jnp.float32)
        for i in range(2 * cper):
            part[i % 2, j * cper + i // 2] = res[i * kb:(i + 1) * kb]
        coef_copy(j).start()
        return carry

    lax.fori_loop(0, ctiles, coef, 0)

    def coef_wait(j, carry):
        coef_copy(j).wait_recv()
        q = pl.ds(j * cper, cper)
        part[core, q] = part[core, q] + half[q]
        return carry

    lax.fori_loop(0, ctiles, coef_wait, 0)

    units = min(4, kb // 8)
    hk = kb // units

    def rs_copy(s, u):
        q = chip_at(pos - step_dir * (1 + s))
        return remote(
            part.at[core, q, pl.ds(u * hk, hk)], sums.at[s, pl.ds(u * hk, hk)],
            ss_sem.at[units * s + u], sr_sem.at[units * s + u], nxt,
        )

    for u in range(units):
        rs_copy(0, u).start()

    def rs_step(s, carry):
        q = chip_at(pos - step_dir * (1 + s))
        for u in range(units):
            rs_copy(s - 1, u).wait_recv()
            span = pl.ds(u * hk, hk)
            part[core, q, span] = part[core, q, span] + sums[s - 1, span]
            rs_copy(s, u).start()
        return carry

    lax.fori_loop(1, nc - 1, rs_step, 0)

    def tm_copy(u):
        span = pl.ds(u * hk, hk)
        return remote(part.at[core, chip, span], twin.at[span], ts_sem.at[u], tr_sem.at[u], other)

    for u in range(units):
        rs_copy(nc - 2, u).wait_recv()
        span = pl.ds(u * hk, hk)
        part[core, chip, span] = part[core, chip, span] + sums[nc - 2, span]
        tm_copy(u).start()
    scale = 1.0 / nr
    for u in range(units):
        tm_copy(u).wait_recv()
        span = pl.ds(u * hk, hk)
        mine = w_ref[tm, tm] * part[core, chip, span]
        out_ref[0, span] = scale * (mine + w_ref[tm, 1 - tm] * twin[span])

    def drain(s, carry):
        for u in range(2):
            @pl.when(s < nc - 1)
            def _():
                g_ring(s, u).wait_send()

            g_loc(s, u, core).wait_send()
        for u in range(units):
            @pl.when(s < nc - 1)
            def _():
                rs_copy(s, u).wait_send()

        @pl.when(s < nh)
        def _():
            for u in range(2):
                b_ring(s, u, s).wait_send()
            for u in range(3):
                b_loc(s, u, core).wait_send()
            b_x(s + 1, 0).wait_send()

        return carry

    lax.fori_loop(0, nc, drain, 0)

    def drain_coef(j, carry):
        coef_copy(j).wait_send()
        return carry

    lax.fori_loop(0, ctiles, drain_coef, 0)
    for u in range(units):
        tm_copy(u).wait_send()


def shards(occupied_green, empty_green, basis, time_weights):
    n = lax.axis_size("grid")
    nc = n // 2
    rows, nb = basis.shape
    kb = occupied_green.shape[1]
    dma = pltpu.SemaphoreType.DMA
    sizes = [3, 2 * nc, 2 * nc, 2 * nc, 2 * nc, 2 * nc, 2 * nc, nc, nc, 3 * nc, 3 * nc]
    sizes += [nc, nc, 4 * nc, 4 * nc, 4, 4]
    any_space = pl.BlockSpec(memory_space=pl.ANY)
    return pl.pallas_call(
        functools.partial(kernel, nc, n * rows),
        out_shape=jax.ShapeDtypeStruct((1, kb, nb), jnp.float32),
        in_specs=[any_space, any_space, any_space, pl.BlockSpec(memory_space=pltpu.SMEM)],
        out_specs=pl.BlockSpec(memory_space=pltpu.VMEM),
        scratch_shapes=[
            pltpu.VMEM((n, rows, nb), jnp.bfloat16),
            pltpu.VMEM((n, 2, kb, nb), jnp.bfloat16),
            pltpu.VMEM((2, rows, nb), jnp.bfloat16),
            pltpu.VMEM((rows, nb), jnp.float32),
            pltpu.VMEM((2, rows, nb), jnp.bfloat16),
            pltpu.VMEM((2, nc, kb, nb), jnp.float32),
            pltpu.VMEM((nc, kb, nb), jnp.float32),
            pltpu.VMEM((nc - 1, kb, nb), jnp.float32),
            pltpu.VMEM((kb, nb), jnp.float32),
        ]
        + [dma((k,)) for k in sizes],
        compiler_params=pltpu.CompilerParams(
            collective_id=0, has_side_effects=True, vmem_limit_bytes=67043328
        ),
    )(occupied_green, empty_green, basis, time_weights)


def solution(mesh):
    in_specs = (P("tm", "grid", None), P("tm", "grid", None), P("grid", None), P())
    out_specs = P("tm", "grid", None)
    return jax.shard_map(shards, mesh=mesh, in_specs=in_specs, out_specs=out_specs, check_vma=False)
```

```python
import functools

import jax
import jax.numpy as jnp
from jax import lax
from jax.experimental import pallas as pl
from jax.experimental.pallas import tpu as pltpu
from jax.sharding import PartitionSpec as P

MESH = pl.DeviceIdType.MESH
NT = (((1,), (1,)), ((), ()))
TN = (((0,), (0,)), ((), ()))


def tile_of(total, most):
    return max(d for d in range(1, most + 1) if total % d == 0)


def kernel(
    nc, nr, occ_ref, emp_ref, basis_ref, w_ref, out_ref,
    full, green, proj, acc, back, part, half, sums, twin,
    load_sem, gs_ring, gr_ring, gs_loc, gr_loc,
    s_ring, r_ring, s_x, r_x, s_loc, r_loc,
    cs_sem, cr_sem, ss_sem, sr_sem, ts_sem, tr_sem,
):
    tm = lax.axis_index("tm")
    me = lax.axis_index("grid")
    rows, nb = basis_ref.shape
    kb = occ_ref.shape[1]
    core = lax.rem(me, 2)
    chip = me // 2
    side = lax.rem(chip, 2)
    lane = chip // 2
    pos = (1 - side) * lane + side * (nc - 1 - lane)
    step_dir = 1 - 2 * core

    def chip_at(position):
        q = lax.rem(position + 2 * nc, nc)
        far = q // (nc // 2)
        return (1 - far) * 2 * q + far * (2 * (nc - 1 - q) + 1)

    def block_at(hops, which_core):
        direction = 1 - 2 * which_core
        return 2 * chip_at(pos - direction * hops) + which_core

    nxt = (tm, 2 * chip_at(pos + step_dir) + core)
    prv = (tm, 2 * chip_at(pos - step_dir) + core)
    mate = (tm, me + step_dir)
    other = (1 - tm, me)
    mate_core = 1 - core

    def remote(src, dst, send, recv, dev):
        return pltpu.make_async_remote_copy(
            src_ref=src, dst_ref=dst, send_sem=send, recv_sem=recv, device_id=dev, device_id_type=MESH
        )

    loads = [
        pltpu.make_async_copy(occ_ref.at[0], green.at[me, 0], load_sem.at[0]),
        pltpu.make_async_copy(emp_ref.at[0], green.at[me, 1], load_sem.at[1]),
        pltpu.make_async_copy(basis_ref, full.at[me], load_sem.at[2]),
    ]
    for load in loads:
        load.start()

    barrier = pltpu.get_barrier_semaphore()
    for peer in (nxt, prv, mate, other):
        pl.semaphore_signal(barrier, inc=1, device_id=peer, device_id_type=MESH)
    pl.semaphore_wait(barrier, 4)

    def g_ring(hops, u):
        b = block_at(hops, core)
        return remote(green.at[b, u], green.at[b, u], gs_ring.at[2 * hops + u], gr_ring.at[2 * hops + u], nxt)

    def g_loc(hops, u, which_core):
        b = block_at(hops, which_core)
        return remote(green.at[b, u], green.at[b, u], gs_loc.at[2 * hops + u], gr_loc.at[2 * hops + u], mate)

    def g_arrived(hops, u):
        b = block_at(hops, core)
        return remote(
            green.at[b, u], green.at[b, u], gs_ring.at[2 * (hops - 1) + u], gr_ring.at[2 * (hops - 1) + u], nxt
        )

    third = rows // 3
    nh = nc // 2

    def piece(b, t):
        return full.at[b, pl.ds(pl.multiple_of(t * third, 16), third)]

    def third_of(u):
        return (2 * tm, 1, 2 - 2 * tm)[u]

    chunk = max(16, 2 * third // nc)
    per_unit = third // chunk

    def own_chunk(c):
        u = c // per_unit
        first = (2 * tm * (1 - u) + u) * third + lax.rem(c, per_unit) * chunk
        ref = full.at[me, pl.ds(pl.multiple_of(first, 16), chunk)]
        remote(ref, ref, s_ring.at[u], r_ring.at[u], nxt).start()

    def b_ring(hops, u, src_hops):
        ref = piece(block_at(src_hops, core), third_of(u))
        return remote(ref, ref, s_ring.at[2 * hops + u], r_ring.at[2 * hops + u], nxt)

    def b_x(hops, u):
        ref = piece(block_at(hops, core), third_of(u))
        return remote(ref, ref, s_x.at[hops], r_x.at[hops], other)

    def b_loc(hops, u, which_core):
        ref = piece(block_at(hops, which_core), third_of(u))
        return remote(ref, ref, s_loc.at[3 * hops + u], r_loc.at[3 * hops + u], mate)

    for u in range(2):
        loads[u].wait()
        g_ring(0, u).start()
        g_loc(0, u, core).start()
    loads[2].wait()
    for u in range(3):
        b_loc(0, u, core).start()
    own_chunk(jnp.int32(0))

    def g_step(s, carry):
        for u in range(2):
            g_arrived(s, u).wait_recv()

            @pl.when(s < nc - 1)
            def _():
                g_ring(s, u).start()

            g_loc(s, u, core).start()

        @pl.when(s < 2 * per_unit)
        def _():
            own_chunk(s)

        return carry

    lax.fori_loop(1, nc, g_step, 0)

    def ring_in(s, u):
        b_ring(s - 1, u, s).wait_recv()

        @pl.when(s < nh)
        def _():
            b_ring(s, u, s).start()
            b_loc(s, u, core).start()

        if u == 0:
            b_x(s, 0).start()

    for u in range(2):
        ring_in(1, u)

    def g_local(s, carry):
        for u in range(2):
            g_loc(s, u, mate_core).wait_recv()
        return carry

    lax.fori_loop(0, nc, g_local, 0)

    per = tile_of(2 * nc, max(1, 512 // kb))
    tiles = 2 * nc // per

    def project(b, i):
        f = i // tiles
        j = lax.rem(i, tiles)
        g = green[pl.ds(j * per, per), f].reshape(per * kb, nb)
        res = lax.dot_general(full[b], g, NT, preferred_element_type=jnp.float32)
        proj[f, :, pl.ds(pl.multiple_of(j * per * kb, 128), per * kb)] = res.astype(jnp.bfloat16)


    tile = tile_of(rows, 768)

    def terms(sub):
        occ = lax.dot_general(proj[0], sub, NT, preferred_element_type=jnp.float32)
        emp = lax.dot_general(proj[1], sub, NT, preferred_element_type=jnp.float32)
        product = (occ * emp).astype(jnp.bfloat16)
        acc[...] += jnp.dot(product, sub, preferred_element_type=jnp.float32)

    def compute(b):
        for i in range(rows // tile):
            terms(full[b, i * tile:(i + 1) * tile])

    def rows_of(which, carry):
        b = block_at(which * nh, core)

        @pl.when(which == 1)
        def _():
            b_x(nh, 2).wait_recv()

        lax.fori_loop(0, 2 * tiles, lambda i, c: (project(b, i), c)[1], 0)
        acc[...] = jnp.zeros_like(acc)

        def step(s, carry):
            first = which == 0

            @pl.when(first & (s > 0))
            def _():
                b_x(s, 2).wait_recv()
                b_loc(s, 2, core).start()

            compute(block_at(s, core))

            @pl.when(first & (s < nh - 1))
            def _():
                ring_in(s + 2, 0)

            @pl.when(first)
            def _():
                for u in range(3):
                    b_loc(s, u, mate_core).wait_recv()

            compute(block_at(s, mate_core))

            @pl.when(first & (s < nh - 1))
            def _():
                ring_in(s + 2, 1)

            return carry

        lax.fori_loop(0, nh, step, 0)
        back[which] = acc[...].astype(jnp.bfloat16)
        return carry

    lax.fori_loop(0, 2, rows_of, 0)

    cper = tile_of(nc, max(1, 256 // kb))
    ctiles = nc // cper

    def coef_copy(j):
        q = pl.ds(j * cper, cper)
        return remote(part.at[mate_core, q], half.at[q], cs_sem.at[j], cr_sem.at[j], mate)

    def coef(j, carry):
        cols = 2 * cper * kb
        span = pl.ds(pl.multiple_of(j * cols, 128), cols)
        res = lax.dot_general(back[0, :, span], full[me], TN, preferred_element_type=jnp.float32)
        far = full[block_at(nh, core)]
        res += lax.dot_general(back[1, :, span], far, TN, preferred_element_type=jnp.float32)
        for i in range(2 * cper):
            part[i % 2, j * cper + i // 2] = res[i * kb:(i + 1) * kb]
        coef_copy(j).start()
        return carry

    lax.fori_loop(0, ctiles, coef, 0)

    def coef_wait(j, carry):
        coef_copy(j).wait_recv()
        q = pl.ds(j * cper, cper)
        part[core, q] = part[core, q] + half[q]
        return carry

    lax.fori_loop(0, ctiles, coef_wait, 0)

    units = min(4, kb // 8)
    hk = kb // units

    def rs_copy(s, u):
        q = chip_at(pos - step_dir * (1 + s))
        return remote(
            part.at[core, q, pl.ds(u * hk, hk)], sums.at[s, pl.ds(u * hk, hk)],
            ss_sem.at[units * s + u], sr_sem.at[units * s + u], nxt,
        )

    for u in range(units):
        rs_copy(0, u).start()

    def rs_step(s, carry):
        q = chip_at(pos - step_dir * (1 + s))
        for u in range(units):
            rs_copy(s - 1, u).wait_recv()
            span = pl.ds(u * hk, hk)
            part[core, q, span] = part[core, q, span] + sums[s - 1, span]
            rs_copy(s, u).start()
        return carry

    lax.fori_loop(1, nc - 1, rs_step, 0)

    def tm_copy(u):
        span = pl.ds(u * hk, hk)
        return remote(part.at[core, chip, span], twin.at[span], ts_sem.at[u], tr_sem.at[u], other)

    for u in range(units):
        rs_copy(nc - 2, u).wait_recv()
        span = pl.ds(u * hk, hk)
        part[core, chip, span] = part[core, chip, span] + sums[nc - 2, span]
        tm_copy(u).start()
    scale = 1.0 / nr
    for u in range(units):
        tm_copy(u).wait_recv()
        span = pl.ds(u * hk, hk)
        mine = w_ref[tm, tm] * part[core, chip, span]
        out_ref[0, span] = scale * (mine + w_ref[tm, 1 - tm] * twin[span])

    def drain(s, carry):
        for u in range(2):
            @pl.when(s < nc - 1)
            def _():
                g_ring(s, u).wait_send()

            g_loc(s, u, core).wait_send()
        for u in range(units):
            @pl.when(s < nc - 1)
            def _():
                rs_copy(s, u).wait_send()

        @pl.when(s < nh)
        def _():
            for u in range(2):
                b_ring(s, u, s).wait_send()
            for u in range(3):
                b_loc(s, u, core).wait_send()
            b_x(s + 1, 0).wait_send()

        return carry

    lax.fori_loop(0, nc, drain, 0)

    def drain_coef(j, carry):
        coef_copy(j).wait_send()
        return carry

    lax.fori_loop(0, ctiles, drain_coef, 0)
    for u in range(units):
        tm_copy(u).wait_send()


def shards(occupied_green, empty_green, basis, time_weights):
    n = lax.axis_size("grid")
    nc = n // 2
    rows, nb = basis.shape
    kb = occupied_green.shape[1]
    dma = pltpu.SemaphoreType.DMA
    sizes = [3, 2 * nc, 2 * nc, 2 * nc, 2 * nc, 2 * nc, 2 * nc, nc, nc, 3 * nc, 3 * nc]
    sizes += [nc, nc, 4 * nc, 4 * nc, 4, 4]
    any_space = pl.BlockSpec(memory_space=pl.ANY)
    return pl.pallas_call(
        functools.partial(kernel, nc, n * rows),
        out_shape=jax.ShapeDtypeStruct((1, kb, nb), jnp.float32),
        in_specs=[any_space, any_space, any_space, pl.BlockSpec(memory_space=pltpu.SMEM)],
        out_specs=pl.BlockSpec(memory_space=pltpu.VMEM),
        scratch_shapes=[
            pltpu.VMEM((n, rows, nb), jnp.bfloat16),
            pltpu.VMEM((n, 2, kb, nb), jnp.bfloat16),
            pltpu.VMEM((2, rows, nb), jnp.bfloat16),
            pltpu.VMEM((rows, nb), jnp.float32),
            pltpu.VMEM((2, rows, nb), jnp.bfloat16),
            pltpu.VMEM((2, nc, kb, nb), jnp.float32),
            pltpu.VMEM((nc, kb, nb), jnp.float32),
            pltpu.VMEM((nc - 1, kb, nb), jnp.float32),
            pltpu.VMEM((kb, nb), jnp.float32),
        ]
        + [dma((k,)) for k in sizes],
        compiler_params=pltpu.CompilerParams(
            collective_id=0, has_side_effects=True, vmem_limit_bytes=67043328
        ),
    )(occupied_green, empty_green, basis, time_weights)


def solution(mesh):
    in_specs = (P("tm", "grid", None), P("tm", "grid", None), P("grid", None), P())
    out_specs = P("tm", "grid", None)
    return jax.shard_map(shards, mesh=mesh, in_specs=in_specs, out_specs=out_specs, check_vma=False)
```
